32 devices in a mesh: dp: 2 (over core), expert: 4 (over y, x), tensor: 4 (over z).
Axes of the slice: x: 2, y: 2, z: 4, core: 2. Of those that a mesh axis runs over, the one named last changes fastest.
Arguments:
- grad_out: bfloat16 [1024, 3584], P(('dp', 'expert')), may hold values from -6 to 6
- layer_in: bfloat16 [1024, 3584], P(('dp', 'expert')), may hold values from -6 to 6
- routes: int32 [1024, 8], P(('dp', 'expert')), may hold values from 0 to 255, as said below
- combine: float32 [1024, 8], P(('dp', 'expert')), may hold values from 0.2 to 1
- gate_weight: bfloat16 [4, 3584, 1024], P('expert', 'dp', 'tensor'), may hold values from -0.09375 to 0.09375
- up_weight: bfloat16 [4, 3584, 1024], P('expert', 'dp', 'tensor'), may hold values from -0.09375 to 0.09375
- down_weight: bfloat16 [4, 1024, 3584], P('expert', 'tensor', 'dp'), may hold values from -0.1875 to 0.1875
Outputs:
- grad_in: bfloat16 [1024, 3584], P(('dp', 'expert'))
- grad_gate: bfloat16 [4, 3584, 1024], P('expert', 'dp', 'tensor')
- grad_up: bfloat16 [4, 3584, 1024], P('expert', 'dp', 'tensor')
- grad_down: bfloat16 [4, 1024, 3584], P('expert', 'tensor', 'dp')
The draws below stay inside these ranges and needn't reach their ends.
Inputs may be any that keep to these rules, and one draw needn't show every extreme that they name: `routes`: each row names 8 different experts. In every block of 128 tokens (the tokens of one device) each expert below 4 is named by 1 to 8 tokens, and one such expert, the same for all blocks of a draw, is named by exactly 8 tokens of every block.
All inputs are finite; a program needn't handle non-finite values.
Results may differ from the reference program's by a relative error of at most 0.011.
Values may be sent and summed in bfloat16 or wider, within the bound.
A program may use at most 128 MiB of HBM per device.

```python
import jax
import jax.numpy as jnp
from jax import lax

D = 3584
FF = 1024
ROUTED = 256
TOP = 8
TOK_DEV = 128
CAP = 8
EXPERTS = 4
TOKENS = 1024
N_DP = 2
N_EXPERT = 4
N_TENSOR = 4


def draw_routes(key, part):
    blocks = TOKENS // TOK_DEV
    subkeys = jax.random.split(jax.random.fold_in(key, 17), 5)
    labels = jnp.arange(EXPERTS, dtype=jnp.int32)
    lowest = max(CAP // 3, 1)
    counts = jax.random.randint(subkeys[0], (blocks, EXPERTS), lowest, CAP + 1).astype(jnp.int32)
    fullest = jax.random.randint(subkeys[1], (), 0, EXPERTS).astype(jnp.int32)
    counts = jnp.where(labels[None, :] == fullest, CAP, counts).astype(jnp.int32)
    residue = labels % TOP
    earlier = ((residue[:, None] == residue[None, :]) & (labels[:, None] < labels[None, :])).astype(jnp.int32)
    starts = jnp.sum(counts[:, :, None] * earlier[None, :, :], axis=1).astype(jnp.int32)
    scores = jax.random.randint(subkeys[2], (blocks, TOP, TOK_DEV), 0, 2 ** 20).astype(jnp.int32) * TOK_DEV + jnp.arange(TOK_DEV, dtype=jnp.int32)
    ranking = jnp.argsort(jnp.argsort(scores, axis=2), axis=2).astype(jnp.int32)
    rank_expert = jnp.take(ranking, residue, axis=1)
    inside = (rank_expert >= starts[:, :, None]) & (rank_expert < (starts + counts)[:, :, None])
    member = (residue[:, None] == jnp.arange(TOP, dtype=jnp.int32)[None, :]).astype(jnp.int32)
    inside_ints = jnp.transpose(inside.astype(jnp.int32), (0, 2, 1))
    found_one = jnp.sum(inside_ints[:, :, :, None] * member[None, None, :, :], axis=2)
    chosen_ids = jnp.sum((inside_ints * labels[None, None, :])[:, :, :, None] * member[None, None, :, :], axis=2)
    spare_ids = ROUTED - EXPERTS
    offset = jax.random.randint(subkeys[3], (blocks, TOK_DEV, 1), 0, spare_ids).astype(jnp.int32)
    others = EXPERTS + (offset + jnp.arange(TOP, dtype=jnp.int32)[None, None, :]) % spare_ids
    expert_ids = jnp.where(found_one > 0, chosen_ids, others).astype(jnp.int32)
    order_scores = jax.random.randint(subkeys[4], (blocks, TOK_DEV, TOP), 0, 2 ** 20).astype(jnp.int32) * TOP + jnp.arange(TOP, dtype=jnp.int32)
    shuffle = jnp.argsort(order_scores, axis=2)
    expert_ids = jnp.take_along_axis(expert_ids, shuffle, axis=2)
    return expert_ids.reshape(TOKENS, TOP).astype(jnp.int32)


def shard_levels(key, extent, shards, smallest, largest):
    level, own = 1.0, jax.random.fold_in(key, 6)
    for dim, parts in shards:
        heights = jnp.exp(jax.random.uniform(jax.random.fold_in(own, dim), (parts,), jnp.float32, smallest / len(shards), largest / len(shards)))
        level = level * jnp.repeat(heights, extent[dim] // parts).reshape([-1 if axis == dim else 1 for axis in range(len(extent))])
    return level


def centred(key, extent, spread, reach, cuts=(), kind=jnp.bfloat16):
    result = spread * jax.random.normal(key, extent, jnp.float32)
    if cuts:
        result = result * shard_levels(key, extent, cuts, -0.22, 0.18)
    return jnp.clip(result, -reach, reach).astype(kind)


def setup_inputs(seed: int = 0) -> dict:
    arg_keys = jax.random.split(jax.random.key(seed), 8)
    return {
        "grad_out": centred(arg_keys[0], (TOKENS, D), 1.0, 6.0, ((0, 8),)),
        "layer_in": centred(arg_keys[1], (TOKENS, D), 1.0, 6.0, ((0, 8),)),
        "routes": draw_routes(jax.random.fold_in(arg_keys[7], 71), 0),
        "combine": jnp.clip(0.2 + 0.8 * jax.random.uniform(arg_keys[3], (TOKENS, TOP), jnp.float32) ** shard_levels(arg_keys[3], (TOKENS, TOP), ((0, 8),), -0.2, 0.2), 0.2, 1.0),
        "gate_weight": centred(arg_keys[4], (EXPERTS, D, FF), D ** -0.5, 0.09375, ((0, 4), (1, 2), (2, 4))),
        "up_weight": centred(arg_keys[5], (EXPERTS, D, FF), D ** -0.5, 0.09375, ((0, 4), (1, 2), (2, 4))),
        "down_weight": centred(arg_keys[6], (EXPERTS, FF, D), FF ** -0.5, 0.1875, ((0, 4), (1, 4), (2, 2))),
    }


def expert_backward(in_rows, grad_rows, gate_w, up_w, down_w):
    gate = jnp.dot(in_rows, gate_w, preferred_element_type=jnp.float32)
    up = jnp.dot(in_rows, up_w, preferred_element_type=jnp.float32)
    sigma = jax.nn.sigmoid(gate)
    silu_gate = gate * sigma
    act = (silu_gate * up).astype(jnp.bfloat16)
    dhid = lax.dot_general(grad_rows, down_w, (((1,), (1,)), ((), ())), preferred_element_type=jnp.float32)
    d_up = (dhid * silu_gate).astype(jnp.bfloat16)
    d_gate = (dhid * up * sigma * (1.0 + gate * (1.0 - sigma))).astype(jnp.bfloat16)
    return act, d_gate, d_up


def reference(grad_out, layer_in, routes, combine, gate_weight, up_weight, down_weight):
    experts = gate_weight.shape[0]
    tokens, width = grad_out.shape
    blocks = tokens // TOK_DEV
    labels = jnp.arange(experts, dtype=jnp.int32)
    hits = routes[:, :, None] == labels[None, None, :]
    chosen = jnp.sum(hits, axis=1, dtype=jnp.int32)
    per_block = chosen.reshape(blocks, TOK_DEV, experts)
    before = (jnp.cumsum(per_block, axis=1) - per_block).reshape(tokens, experts).astype(jnp.int32)
    block_of = jnp.arange(tokens, dtype=jnp.int32) // TOK_DEV
    slot_of = (labels[None, :] * blocks + block_of[:, None]) * CAP + before
    dump_row = experts * blocks * CAP
    target = jnp.where(chosen > 0, slot_of, dump_row).astype(jnp.int32)
    token_ids = jnp.broadcast_to(jnp.arange(tokens, dtype=jnp.int32)[:, None] + 1, target.shape)
    owner = jnp.zeros((dump_row + 1,), jnp.int32).at[target.reshape(-1)].set(token_ids.reshape(-1))[:dump_row] - 1
    scale_of = jnp.sum(jnp.where(hits, combine[:, :, None], jnp.zeros((), jnp.float32)), axis=1)
    factor = jnp.zeros((dump_row + 1,), jnp.float32).at[target.reshape(-1)].set(scale_of.reshape(-1))[:dump_row]
    owner = owner.reshape(experts, blocks * CAP)
    factor = factor.reshape(experts, blocks * CAP)
    group_width = FF // N_TENSOR
    replica_rows = N_EXPERT * CAP

    def one_expert(items):
        owner_row, factor_row, gate_w, up_w, down_w = items
        valid = owner_row >= 0
        safe = jnp.maximum(owner_row, 0)
        in_rows = jnp.where(valid[:, None], layer_in[safe], jnp.zeros((), jnp.bfloat16))
        grad_rows = (grad_out[safe].astype(jnp.float32) * factor_row[:, None]).astype(jnp.bfloat16)
        act, d_gate, d_up = expert_backward(in_rows, grad_rows, gate_w, up_w, down_w)
        row_total = jnp.zeros(in_rows.shape, jnp.float32)
        for group in range(N_TENSOR):
            lo_col = group * group_width
            term = lax.dot_general(d_gate[:, lo_col:lo_col + group_width], gate_w[:, lo_col:lo_col + group_width], (((1,), (1,)), ((), ())), preferred_element_type=jnp.float32)
            term = term + lax.dot_general(d_up[:, lo_col:lo_col + group_width], up_w[:, lo_col:lo_col + group_width], (((1,), (1,)), ((), ())), preferred_element_type=jnp.float32)
            row_total = row_total + lax.optimization_barrier(term.astype(jnp.bfloat16)).astype(jnp.float32)
        gate_total = jnp.zeros(gate_w.shape, jnp.float32)
        up_total = jnp.zeros(up_w.shape, jnp.float32)
        down_total = jnp.zeros(down_w.shape, jnp.float32)
        for replica in range(N_DP):
            lo_row = replica * replica_rows
            rows_in = in_rows[lo_row:lo_row + replica_rows]
            part_gate = lax.dot_general(rows_in, d_gate[lo_row:lo_row + replica_rows], (((0,), (0,)), ((), ())), preferred_element_type=jnp.float32) * 0.25
            part_up = lax.dot_general(rows_in, d_up[lo_row:lo_row + replica_rows], (((0,), (0,)), ((), ())), preferred_element_type=jnp.float32) * 0.25
            part_down = lax.dot_general(act[lo_row:lo_row + replica_rows], grad_rows[lo_row:lo_row + replica_rows], (((0,), (0,)), ((), ())), preferred_element_type=jnp.float32) * 0.25
            gate_total = gate_total + lax.optimization_barrier(part_gate.astype(jnp.bfloat16)).astype(jnp.float32)
            up_total = up_total + lax.optimization_barrier(part_up.astype(jnp.bfloat16)).astype(jnp.float32)
            down_total = down_total + lax.optimization_barrier(part_down.astype(jnp.bfloat16)).astype(jnp.float32)
        return (row_total.astype(jnp.bfloat16), gate_total.astype(jnp.bfloat16), up_total.astype(jnp.bfloat16), down_total.astype(jnp.bfloat16))

    rows_all, grad_gate, grad_up, grad_down = lax.map(one_expert, (owner, factor, gate_weight, up_weight, down_weight))
    pair_pos = jnp.sum(jnp.where(hits, slot_of[:, None, :], 0), axis=2) + dump_row * (1 - jnp.sum(hits, axis=2, dtype=jnp.int32))
    pair_pos = pair_pos.astype(jnp.int32)
    row_table = jnp.concatenate([rows_all.reshape(dump_row, width), jnp.zeros((1, width), jnp.bfloat16)], axis=0)
    total = jnp.zeros((tokens, width), jnp.float32)
    for choice_index in range(TOP):
        total = total + row_table[pair_pos[:, choice_index]].astype(jnp.float32)
    return (total.astype(jnp.bfloat16), grad_gate, grad_up, grad_down)
```

```python
import jax
import jax.numpy as jnp
from jax import lax
from jax.experimental import pallas as pl
from jax.experimental.pallas import tpu as pltpu
from jax.sharding import PartitionSpec as P

CAP = 8
MESH = pl.DeviceIdType.MESH
F32 = jnp.float32
BF16 = jnp.bfloat16


def dot(a, b, ca, cb):
    return lax.dot_general(a, b, (((ca,), (cb,)), ((), ())), preferred_element_type=F32)


def make_kernel(nd, ne, nz, tokens, width, half, hidden, top, chunks):
    ni = ne // nz
    order = [z + nz * i for z in range(nz) for i in range(ni)]
    place = {k: p for p, k in enumerate(order)}
    lanes = ne * CAP
    rows = ne * nd * CAP
    wide = half // chunks

    def kernel(
        go_hbm, li_hbm, routes_ref, combine_ref, gw_hbm, uw_hbm, dw_hbm,
        out_ref, gg_ref, gu_ref, gd_ref,
        go, li, gw, uw, dw, send, recv, psend, precv, rowg, rsrecv, retsend, agbuf,
        ld_sem, out_sem, d_send, d_recv, p_send, p_recv, r_send, r_recv,
        t_send, t_recv, a_send, a_recv,
        gg_v, gu_v, gd_v, out_v,
    ):
        d = lax.axis_index("dp")
        e = lax.axis_index("expert")
        z = lax.axis_index("tensor")

        loads = [
            pltpu.make_async_copy(li_hbm, li, ld_sem.at[0]),
            pltpu.make_async_copy(go_hbm, go, ld_sem.at[1]),
            pltpu.make_async_copy(gw_hbm.at[0], gw, ld_sem.at[2]),
            pltpu.make_async_copy(uw_hbm.at[0], uw, ld_sem.at[3]),
            pltpu.make_async_copy(dw_hbm.at[0], dw, ld_sem.at[4]),
        ]
        for c in loads:
            c.start()

        barrier = pltpu.get_barrier_semaphore()
        peers = 0
        for j in range(nd):
            for k in range(ne):
                if j == 0 and k == 0:
                    continue
                pl.semaphore_signal(
                    barrier, inc=1,
                    device_id=(lax.rem(d + j, nd), lax.rem(e + k, ne), z),
                    device_id_type=MESH,
                )
                peers += 1
        for r in range(1, nz):
            pl.semaphore_signal(
                barrier, inc=1, device_id=(d, e, lax.rem(z + r, nz)), device_id_type=MESH
            )
            peers += 1

        lane = lax.broadcasted_iota(jnp.int32, (tokens, lanes), 1)
        group = lane // CAP
        slot = lane - group * CAP
        label = jnp.zeros((tokens, lanes), jnp.int32)
        for p, k in enumerate(order):
            label = jnp.where(group == p, lax.rem(e + k, ne), label)
        chosen = jnp.zeros((tokens, lanes), F32)
        scale = jnp.zeros((tokens, lanes), F32)
        for c in range(top):
            hit = routes_ref[:, c : c + 1] == label
            chosen = chosen + jnp.where(hit, 1.0, 0.0)
            scale = scale + jnp.where(hit, combine_ref[:, c : c + 1], 0.0)
        row_id = lax.broadcasted_iota(jnp.int32, (tokens, tokens), 0)
        col_id = lax.broadcasted_iota(jnp.int32, (tokens, tokens), 1)
        lower = jnp.where(col_id < row_id, 1.0, 0.0).astype(BF16)
        before = dot(lower, chosen.astype(BF16), 1, 0)
        keep = jnp.logical_and(chosen > 0.0, before == slot.astype(F32))
        pick_f = jnp.where(keep, 1.0, 0.0)
        pick = pick_f.astype(BF16)
        factor = jnp.sum(jnp.transpose(pick_f * scale), axis=1, keepdims=True)

        loads[0].wait()
        loads[1].wait()
        pl.semaphore_wait(barrier, peers)

        def block_of(k, j):
            return k * nd + j

        sends = []
        for j in range(nd - 1, -1, -1):
            dj = lax.rem(d + j, nd)
            off = pl.multiple_of(dj * half, 128)
            in_pick = dot(pick, li[:, pl.ds(off, half)], 0, 0)
            gr_pick = dot(pick, go[:, pl.ds(off, half)], 0, 0) * factor
            for k in range(ne - 1, -1, -1):
                lo = place[k] * CAP
                tile = jnp.concatenate(
                    [in_pick[lo : lo + CAP], gr_pick[lo : lo + CAP]], axis=0
                ).astype(BF16)
                b = block_of(k, j)
                if j == 0 and k == 0:
                    recv[b] = tile
                    continue
                send[b] = tile
                c = pltpu.make_async_remote_copy(
                    src_ref=send.at[b], dst_ref=recv.at[b],
                    send_sem=d_send.at[b], recv_sem=d_recv.at[b],
                    device_id=(dj, lax.rem(e + k, ne), z), device_id_type=MESH,
                )
                c.start()
                sends.append((b, c))
        for c in loads[2:]:
            c.wait()
        for b, c in sends:
            c.wait_recv()

        x = recv[...].reshape(ne * nd * 2 * CAP, half)

        def take(v, which):
            v = v.reshape(ne * nd, 2, CAP, hidden)[:, which]
            return v.reshape(rows, hidden)

        gate = take(dot(x, gw[...], 1, 0), 0)
        up = take(dot(x, uw[...], 1, 0), 0)
        dhid = take(dot(x, dw[...], 1, 1), 1)
        psend[0] = gate.astype(psend.dtype)
        psend[1] = up.astype(psend.dtype)
        psend[2] = dhid.astype(psend.dtype)
        pcopies = []
        for j in range(1, nd):
            c = pltpu.make_async_remote_copy(
                src_ref=psend, dst_ref=precv.at[j - 1],
                send_sem=p_send.at[j - 1], recv_sem=p_recv.at[j - 1],
                device_id=(lax.rem(d + j, nd), e, z), device_id_type=MESH,
            )
            c.start()
            pcopies.append(c)

        def swap(v, j):
            v = v.reshape(ne, nd, CAP, hidden)
            parts = [v[:, (q + nd - j) % nd] for q in range(nd)]
            return jnp.stack(parts, axis=1).reshape(rows, hidden)

        for j, c in enumerate(pcopies, start=1):
            c.wait_recv()
            gate = gate + swap(precv[j - 1, 0].astype(F32), j)
            up = up + swap(precv[j - 1, 1].astype(F32), j)
            dhid = dhid + swap(precv[j - 1, 2].astype(F32), j)

        sigma = jax.nn.sigmoid(gate)
        silu = gate * sigma
        act = silu * up
        d_up = dhid * silu
        d_gate = dhid * up * sigma * (1.0 + gate * (1.0 - sigma))

        row = dot(d_gate.astype(BF16), gw[...], 1, 1) + dot(d_up.astype(BF16), uw[...], 1, 1)
        row = row.astype(BF16).reshape(ne, nd * CAP, half)
        for p, k in enumerate(order):
            rowg[p // ni, p % ni] = row[k]

        rs = []
        for r in range(1, nz):
            zt = lax.rem(z + r, nz)
            c = pltpu.make_async_remote_copy(
                src_ref=rowg.at[zt], dst_ref=rsrecv.at[r - 1],
                send_sem=r_send.at[r - 1], recv_sem=r_recv.at[r - 1],
                device_id=(d, e, zt), device_id_type=MESH,
            )
            c.start()
            rs.append(c)

        def pad(v, which):
            v = v.reshape(ne * nd, CAP, hidden)
            zero = jnp.zeros_like(v)
            pair = [v, zero] if which == 0 else [zero, v]
            return jnp.concatenate(pair, axis=1).reshape(ne * nd * 2 * CAP, hidden).astype(BF16)

        dg_pad = pad(d_gate, 0)
        du_pad = pad(d_up, 0)
        act_pad = pad(act, 1)
        gg_v[...] = (dot(x, dg_pad, 0, 0) * 0.25).astype(BF16)
        o_gg = pltpu.make_async_copy(gg_v, gg_ref.at[0], out_sem.at[0])
        o_gg.start()

        total = rowg[z].astype(F32)
        for r in range(1, nz):
            rs[r - 1].wait_recv()
            total = total + rsrecv[r - 1].astype(F32)
        total = total.reshape(ni, nd, CAP, half)
        retsend[...] = total.astype(BF16)

        def ret_copy(i, j):
            k = z + nz * i
            return pltpu.make_async_remote_copy(
                src_ref=retsend.at[i, j], dst_ref=agbuf.at[z, i, d],
                send_sem=t_send.at[i, j], recv_sem=t_recv.at[i, d],
                device_id=(lax.rem(d + nd - j, nd), lax.rem(e + ne - k, ne), z),
                device_id_type=MESH,
            )

        def own_copy():
            return pltpu.make_async_copy(retsend.at[0, 0], agbuf.at[z, 0, d], t_recv.at[0, d])

        for i in range(ni):
            for j in range(nd):
                if i == 0 and j == 0:
                    @pl.when(z == 0)
                    def _():
                        own_copy().start()

                    @pl.when(z != 0)
                    def _():
                        ret_copy(0, 0).start()
                else:
                    ret_copy(i, j).start()

        gu_v[...] = (dot(x, du_pad, 0, 0) * 0.25).astype(BF16)
        o_gu = pltpu.make_async_copy(gu_v, gu_ref.at[0], out_sem.at[1])
        o_gu.start()

        for i in range(ni):
            for q in range(nd):
                pltpu.make_async_copy(
                    retsend.at[i, q], agbuf.at[z, i, q], t_recv.at[i, q]
                ).wait()
        ag = []
        for r in range(1, nz):
            c = pltpu.make_async_remote_copy(
                src_ref=agbuf.at[z], dst_ref=agbuf.at[z],
                send_sem=a_send.at[r - 1], recv_sem=a_recv.at[r - 1],
                device_id=(d, e, lax.rem(z + r, nz)), device_id_type=MESH,
            )
            c.start()
            ag.append(c)

        gd_v[...] = (dot(act_pad, x, 0, 0) * 0.25).astype(BF16)
        o_gd = pltpu.make_async_copy(gd_v, gd_ref.at[0], out_sem.at[2])
        o_gd.start()

        for r in range(1, nz):
            zs = lax.rem(z + nz - r, nz)
            pltpu.make_async_copy(agbuf.at[zs], agbuf.at[zs], a_recv.at[r - 1]).wait()

        for q in range(nd):
            got = agbuf[:, :, q].astype(F32).reshape(lanes, half).astype(BF16)
            out_v[:, q * half : (q + 1) * half] = dot(pick, got, 1, 0).astype(BF16)
        o_in = pltpu.make_async_copy(out_v, out_ref, out_sem.at[3])
        o_in.start()

        for b, c in sends:
            c.wait_send()
        for c in pcopies:
            c.wait_send()
        for c in rs:
            c.wait_send()
        for i in range(ni):
            for j in range(nd):
                if i == 0 and j == 0:
                    @pl.when(z != 0)
                    def _():
                        ret_copy(0, 0).wait_send()
                else:
                    ret_copy(i, j).wait_send()
        for c in ag:
            c.wait_send()
        for c in (o_gg, o_gu, o_gd, o_in):
            c.wait()

    return kernel


def body(grad_out, layer_in, routes, combine, gate_weight, up_weight, down_weight):
    nd = lax.axis_size("dp")
    ne = lax.axis_size("expert")
    nz = lax.axis_size("tensor")
    tokens, width = grad_out.shape
    top = routes.shape[1]
    half, hidden = gate_weight.shape[1:]
    ni = ne // nz
    blocks = ne * nd
    kernel = make_kernel(nd, ne, nz, tokens, width, half, hidden, top, 1)
    anyspec = pl.BlockSpec(memory_space=pl.ANY)
    vspec = pl.BlockSpec(memory_space=pltpu.VMEM)
    dma = pltpu.SemaphoreType.DMA
    return tuple(
        pl.pallas_call(
            kernel,
            out_shape=(
                jax.ShapeDtypeStruct((tokens, width), BF16),
                jax.ShapeDtypeStruct(gate_weight.shape, BF16),
                jax.ShapeDtypeStruct(up_weight.shape, BF16),
                jax.ShapeDtypeStruct(down_weight.shape, BF16),
            ),
            in_specs=[anyspec, anyspec, vspec, vspec, anyspec, anyspec, anyspec],
            out_specs=(anyspec,) * 4,
            scratch_shapes=[
                pltpu.VMEM((tokens, width), BF16),
                pltpu.VMEM((tokens, width), BF16),
                pltpu.VMEM((half, hidden), BF16),
                pltpu.VMEM((half, hidden), BF16),
                pltpu.VMEM((hidden, half), BF16),
                pltpu.VMEM((blocks, 2 * CAP, half), BF16),
                pltpu.VMEM((blocks, 2 * CAP, half), BF16),
                pltpu.VMEM((3, blocks * CAP, hidden), BF16),
                pltpu.VMEM((nd - 1, 3, blocks * CAP, hidden), BF16),
                pltpu.VMEM((nz, ni, nd * CAP, half), BF16),
                pltpu.VMEM((nz - 1, ni, nd * CAP, half), BF16),
                pltpu.VMEM((ni, nd, CAP, half), BF16),
                pltpu.VMEM((nz, ni, nd, CAP, half), BF16),
                dma((5,)),
                dma((4,)),
                dma((blocks,)),
                dma((blocks,)),
                dma((nd - 1,)),
                dma((nd - 1,)),
                dma((nz - 1,)),
                dma((nz - 1,)),
                dma((ni, nd)),
                dma((ni, nd)),
                dma((nz - 1,)),
                dma((nz - 1,)),
                pltpu.VMEM((half, hidden), BF16),
                pltpu.VMEM((half, hidden), BF16),
                pltpu.VMEM((hidden, half), BF16),
                pltpu.VMEM((tokens, width), BF16),
            ],
            compiler_params=pltpu.CompilerParams(
                collective_id=0, has_side_effects=True, vmem_limit_bytes=60 * 1024 * 1024
            ),
        )(grad_out, layer_in, routes, combine, gate_weight, up_weight, down_weight)
    )


def solution(mesh):
    return jax.shard_map(
        body,
        mesh=mesh,
        in_specs=(
            P(("dp", "expert"), None),
            P(("dp", "expert"), None),
            P(("dp", "expert"), None),
            P(("dp", "expert"), None),
            P("expert", "dp", "tensor"),
            P("expert", "dp", "tensor"),
            P("expert", "tensor", "dp"),
        ),
        out_specs=(
            P(("dp", "expert"), None),
            P("expert", "dp", "tensor"),
            P("expert", "dp", "tensor"),
            P("expert", "tensor", "dp"),
        ),
        check_vma=False,
    )
```

```python
import jax
import jax.numpy as jnp
from jax import lax
from jax.experimental import pallas as pl
from jax.experimental.pallas import tpu as pltpu
from jax.sharding import PartitionSpec as P

CAP = 8
VMEM = 67043328
MESH = pl.DeviceIdType.MESH
F32 = jnp.float32
BF16 = jnp.bfloat16


def dot(a, b, ca, cb):
    return lax.dot_general(a, b, (((ca,), (cb,)), ((), ())), preferred_element_type=F32)


def make_kernel(nd, ne, nz, tokens, width, half, hidden, top, chunks):
    ni = ne // nz
    order = [z + nz * i for z in range(nz) for i in range(ni)]
    place = {k: p for p, k in enumerate(order)}
    lanes = ne * CAP
    rows = ne * nd * CAP
    wide = half // chunks

    def kernel(
        go_hbm, li_hbm, routes_hbm, combine_hbm, gw_hbm, uw_hbm, dw_hbm,
        out_ref, gg_ref, gu_ref, gd_ref,
        go, li, routes, combine, gw, uw, dw, send, recv, psend, precv, rowg, terms, agbuf,
        ld_sem, d_send, d_recv, p_send, p_recv, r_send, r_recv,
        a_send, a_recv,
    ):
        d = lax.axis_index("dp")
        e = lax.axis_index("expert")
        z = lax.axis_index("tensor")

        loads = [
            pltpu.make_async_copy(li_hbm, li, ld_sem.at[0]),
            pltpu.make_async_copy(go_hbm, go, ld_sem.at[1]),
            pltpu.make_async_copy(gw_hbm.at[0], gw, ld_sem.at[2]),
            pltpu.make_async_copy(uw_hbm.at[0], uw, ld_sem.at[3]),
            pltpu.make_async_copy(dw_hbm.at[0], dw, ld_sem.at[4]),
            pltpu.make_async_copy(routes_hbm, routes, ld_sem.at[5]),
            pltpu.make_async_copy(combine_hbm, combine, ld_sem.at[6]),
        ]
        for i in (5, 6, 0, 1, 2, 3, 4):
            loads[i].start()

        barrier = pltpu.get_barrier_semaphore()
        peers = 0
        for j in range(nd):
            for k in range(ne):
                for r in range(nz):
                    if j == 0 and k == 0 and r == 0:
                        continue
                    pl.semaphore_signal(
                        barrier, inc=1,
                        device_id=(lax.rem(d + j, nd), lax.rem(e + k, ne), lax.rem(z + r, nz)),
                        device_id_type=MESH,
                    )
                    peers += 1

        row = lax.broadcasted_iota(jnp.int32, (lanes, tokens), 0)
        group = row // CAP
        slot = row - group * CAP
        label = jnp.zeros((lanes, tokens), jnp.int32)
        for p, k in enumerate(order):
            label = jnp.where(group == p, lax.rem(e + k, ne), label)
        chosen = jnp.zeros((lanes, tokens), F32)
        scale = jnp.zeros((lanes, tokens), F32)
        loads[5].wait()
        loads[6].wait()
        for c in range(top):
            hit = routes[c : c + 1, :] == label
            chosen = chosen + jnp.where(hit, 1.0, 0.0)
            scale = scale + jnp.where(hit, combine[c : c + 1, :], 0.0)
        row_id = lax.broadcasted_iota(jnp.int32, (tokens, tokens), 0)
        col_id = lax.broadcasted_iota(jnp.int32, (tokens, tokens), 1)
        upper = jnp.where(row_id < col_id, 1.0, 0.0).astype(BF16)
        before = dot(chosen.astype(BF16), upper, 1, 0)
        keep = jnp.logical_and(chosen > 0.0, before == slot.astype(F32))
        pick_f = jnp.where(keep, 1.0, 0.0)
        pick = pick_f.astype(BF16)
        factor = jnp.sum(pick_f * scale, axis=1, keepdims=True)

        loads[0].wait()
        loads[1].wait()
        pl.semaphore_wait(barrier, peers)

        def block_of(k, j):
            return k * nd + j

        sends = []
        for j in range(nd - 1, -1, -1):
            dj = lax.rem(d + j, nd)
            off = pl.multiple_of(dj * half, 128)
            in_pick = dot(pick, li[:, pl.ds(off, half)], 1, 0)
            gr_pick = dot(pick, go[:, pl.ds(off, half)], 1, 0) * factor
            for k in range(ne - 1, -1, -1):
                lo = place[k] * CAP
                tile = jnp.concatenate(
                    [in_pick[lo : lo + CAP], gr_pick[lo : lo + CAP]], axis=0
                ).astype(BF16)
                b = block_of(k, j)
                if j == 0 and k == 0:
                    recv[b] = tile
                    continue
                send[b] = tile
                c = pltpu.make_async_remote_copy(
                    src_ref=send.at[b], dst_ref=recv.at[b],
                    send_sem=d_send.at[b], recv_sem=d_recv.at[b],
                    device_id=(dj, lax.rem(e + k, ne), z), device_id_type=MESH,
                )
                c.start()
                sends.append((b, c))
        for c in loads[2:5]:
            c.wait()
        for b, c in sends:
            c.wait_recv()

        x = recv[...].reshape(ne * nd * 2 * CAP, half)

        def take(v, which):
            v = v.reshape(ne * nd, 2, CAP, hidden)[:, which]
            return v.reshape(rows, hidden)

        gate = take(dot(x, gw[...], 1, 0), 0)
        up = take(dot(x, uw[...], 1, 0), 0)
        dhid = take(dot(x, dw[...], 1, 1), 1)
        psend[0] = gate.astype(psend.dtype)
        psend[1] = up.astype(psend.dtype)
        psend[2] = dhid.astype(psend.dtype)
        pcopies = []
        for j in range(1, nd):
            c = pltpu.make_async_remote_copy(
                src_ref=psend, dst_ref=precv.at[j - 1],
                send_sem=p_send.at[j - 1], recv_sem=p_recv.at[j - 1],
                device_id=(lax.rem(d + j, nd), e, z), device_id_type=MESH,
            )
            c.start()
            pcopies.append(c)

        def swap(v, j):
            v = v.reshape(ne, nd, CAP, hidden)
            parts = [v[:, (q + nd - j) % nd] for q in range(nd)]
            return jnp.stack(parts, axis=1).reshape(rows, hidden)

        for j, c in enumerate(pcopies, start=1):
            c.wait_recv()
            gate = gate + swap(precv[j - 1, 0].astype(F32), j)
            up = up + swap(precv[j - 1, 1].astype(F32), j)
            dhid = dhid + swap(precv[j - 1, 2].astype(F32), j)

        sigma = jax.nn.sigmoid(gate)
        silu = gate * sigma
        act = silu * up
        d_up = dhid * silu
        d_gate = dhid * up * sigma * (1.0 + gate * (1.0 - sigma))

        grad = dot(d_gate.astype(BF16), gw[...], 1, 1) + dot(d_up.astype(BF16), uw[...], 1, 1)
        grad = grad.reshape(ne, nd, CAP, half)
        for k in range(ne):
            for j in range(nd):
                rowg[k, j] = grad[k, j].astype(BF16)

        def term_copy(k, j):
            return pltpu.make_async_remote_copy(
                src_ref=rowg.at[k, j], dst_ref=terms.at[z, k // nz, d],
                send_sem=r_send.at[k, j], recv_sem=r_recv.at[z, k // nz, d],
                device_id=(lax.rem(d + nd - j, nd), lax.rem(e + ne - k, ne), k % nz),
                device_id_type=MESH,
            )

        own = pltpu.make_async_copy(rowg.at[0, 0], terms.at[0, 0, d], r_recv.at[0, 0, d])
        for k in range(ne - 1, -1, -1):
            for j in range(nd):
                if k == 0 and j == 0:
                    @pl.when(z == 0)
                    def _():
                        own.start()

                    @pl.when(z != 0)
                    def _():
                        term_copy(0, 0).start()
                else:
                    term_copy(k, j).start()

        def pad(v, which):
            v = v.reshape(ne * nd, CAP, hidden)
            zero = jnp.zeros_like(v)
            pair = [v, zero] if which == 0 else [zero, v]
            return jnp.concatenate(pair, axis=1).reshape(ne * nd * 2 * CAP, hidden).astype(BF16)

        dg_pad = pad(d_gate, 0)
        du_pad = pad(d_up, 0)
        act_pad = pad(act, 1)
        gg_ref[0] = (dot(x, dg_pad, 0, 0) * 0.25).astype(BF16)
        gu_ref[0] = (dot(x, du_pad, 0, 0) * 0.25).astype(BF16)

        total = jnp.zeros((ni, nd, CAP, half), F32)
        for q in range(nz):
            for i in range(ni):
                for h in range(nd):
                    pltpu.make_async_copy(
                        terms.at[q, i, h], terms.at[q, i, h], r_recv.at[q, i, h]
                    ).wait()
            total = total + terms[q].astype(F32)
        agbuf[z] = total.astype(BF16)
        ag = []
        for r in range(1, nz):
            c = pltpu.make_async_remote_copy(
                src_ref=agbuf.at[z], dst_ref=agbuf.at[z],
                send_sem=a_send.at[r - 1], recv_sem=a_recv.at[r - 1],
                device_id=(d, e, lax.rem(z + r, nz)), device_id_type=MESH,
            )
            c.start()
            ag.append(c)

        gd_ref[0] = (dot(act_pad, x, 0, 0) * 0.25).astype(BF16)
        for r in range(1, nz):
            zs = lax.rem(z + nz - r, nz)
            pltpu.make_async_copy(agbuf.at[zs], agbuf.at[zs], a_recv.at[r - 1]).wait()

        for q in range(nd):
            got = agbuf[:, :, q].astype(F32).reshape(lanes, half).astype(BF16)
            out_ref[:, q * half : (q + 1) * half] = dot(pick, got, 0, 0).astype(BF16)
        for b, c in sends:
            c.wait_send()
        for c in pcopies:
            c.wait_send()
        for k in range(ne):
            for j in range(nd):
                if k == 0 and j == 0:
                    @pl.when(z != 0)
                    def _():
                        term_copy(0, 0).wait_send()
                else:
                    term_copy(k, j).wait_send()
        for c in ag:
            c.wait_send()

    return kernel


def body(grad_out, layer_in, routes, combine, gate_weight, up_weight, down_weight):
    nd = lax.axis_size("dp")
    ne = lax.axis_size("expert")
    nz = lax.axis_size("tensor")
    tokens, width = grad_out.shape
    top = routes.shape[1]
    half, hidden = gate_weight.shape[1:]
    ni = ne // nz
    blocks = ne * nd
    kernel = make_kernel(nd, ne, nz, tokens, width, half, hidden, top, 1)
    hbm = pl.BlockSpec(memory_space=pltpu.HBM)
    vmem = pl.BlockSpec(memory_space=pltpu.VMEM)
    dma = pltpu.SemaphoreType.DMA
    held = 2 * (tokens * width + 3 * half * hidden)
    room = VMEM - held
    parts = pl.pallas_call(
            kernel,
            out_shape=(
                pltpu.VMEM((tokens, width), BF16),
                pltpu.VMEM(gate_weight.shape, BF16),
                pltpu.VMEM(up_weight.shape, BF16),
                pltpu.VMEM(down_weight.shape, BF16),
            ),
            in_specs=[hbm] * 7,
            out_specs=(vmem,) * 4,
            scratch_shapes=[
                pltpu.VMEM((tokens, width), BF16),
                pltpu.VMEM((tokens, width), BF16),
                pltpu.VMEM((top, tokens), jnp.int32),
                pltpu.VMEM((top, tokens), F32),
                pltpu.VMEM((half, hidden), BF16),
                pltpu.VMEM((half, hidden), BF16),
                pltpu.VMEM((hidden, half), BF16),
                pltpu.VMEM((blocks, 2 * CAP, half), BF16),
                pltpu.VMEM((blocks, 2 * CAP, half), BF16),
                pltpu.VMEM((3, blocks * CAP, hidden), BF16),
                pltpu.VMEM((nd - 1, 3, blocks * CAP, hidden), BF16),
                pltpu.VMEM((ne, nd, CAP, half), BF16),
                pltpu.VMEM((nz, ni, nd, CAP, half), BF16),
                pltpu.VMEM((nz, ni, nd, CAP, half), BF16),
                dma((7,)),
                dma((blocks,)),
                dma((blocks,)),
                dma((nd - 1,)),
                dma((nd - 1,)),
                dma((ne, nd)),
                dma((nz, ni, nd)),
                dma((nz - 1,)),
                dma((nz - 1,)),
            ],
            compiler_params=pltpu.CompilerParams(
                collective_id=0, has_side_effects=True, vmem_limit_bytes=room
            ),
        )(grad_out, layer_in, routes.T, combine.T, gate_weight, up_weight, down_weight)
    return tuple(parts)


def solution(mesh):
    return jax.shard_map(
        body,
        mesh=mesh,
        in_specs=(
            P(("dp", "expert"), None),
            P(("dp", "expert"), None),
            P(("dp", "expert"), None),
            P(("dp", "expert"), None),
            P("expert", "dp", "tensor"),
            P("expert", "dp", "tensor"),
            P("expert", "tensor", "dp"),
        ),
        out_specs=(
            P(("dp", "expert"), None),
            P("expert", "dp", "tensor"),
            P("expert", "dp", "tensor"),
            P("expert", "tensor", "dp"),
        ),
        check_vma=False,
    )
```

```python
import jax
import jax.numpy as jnp
from jax import lax
from jax.experimental import pallas as pl
from jax.experimental.pallas import tpu as pltpu
from jax.sharding import PartitionSpec as P

CAP = 8
OUT_PARTS = 2
BACK_PARTS = 2
VMEM = 67043328
MESH = pl.DeviceIdType.MESH
F32 = jnp.float32
BF16 = jnp.bfloat16


def dot(a, b, ca, cb):
    return lax.dot_general(a, b, (((ca,), (cb,)), ((), ())), preferred_element_type=F32)


def cuts(extent, parts):
    tiles = extent // 128
    edges = [128 * ((tiles * c + parts - 1) // parts) for c in range(parts + 1)]
    return list(zip(edges[:-1], edges[1:]))


def make_kernel(nd, ne, nz, tokens, width, half, hidden, top):
    ni = ne // nz
    order = [z + nz * i for z in range(nz) for i in range(ni)]
    place = {k: p for p, k in enumerate(order)}
    lanes = ne * CAP
    rows = ne * nd * CAP
    out_cuts = cuts(half, OUT_PARTS)
    back_cuts = cuts(half, BACK_PARTS)

    def kernel(
        go_hbm, li_hbm, routes_hbm, combine_hbm, gw_hbm, uw_hbm, dw_hbm,
        out_ref, gg_ref, gu_ref, gd_ref,
        go, li, routes, combine, gw, uw, dw, send, recv, psend, precv, rowg, terms, agbuf,
        ld_sem, d_send, d_recv, p_send, p_recv, r_send, r_recv,
        a_send, a_recv,
    ):
        d = lax.axis_index("dp")
        e = lax.axis_index("expert")
        z = lax.axis_index("tensor")

        loads = [
            pltpu.make_async_copy(li_hbm, li, ld_sem.at[0]),
            pltpu.make_async_copy(go_hbm, go, ld_sem.at[1]),
            pltpu.make_async_copy(gw_hbm.at[0], gw, ld_sem.at[2]),
            pltpu.make_async_copy(uw_hbm.at[0], uw, ld_sem.at[3]),
            pltpu.make_async_copy(dw_hbm.at[0], dw, ld_sem.at[4]),
            pltpu.make_async_copy(routes_hbm, routes, ld_sem.at[5]),
            pltpu.make_async_copy(combine_hbm, combine, ld_sem.at[6]),
        ]
        for i in (5, 6, 0, 1, 2, 3, 4):
            loads[i].start()

        barrier = pltpu.get_barrier_semaphore()
        peers = 0
        for j in range(nd):
            for k in range(ne):
                for r in range(nz):
                    if j == 0 and k == 0 and r == 0:
                        continue
                    pl.semaphore_signal(
                        barrier, inc=1,
                        device_id=(lax.rem(d + j, nd), lax.rem(e + k, ne), lax.rem(z + r, nz)),
                        device_id_type=MESH,
                    )
                    peers += 1

        row = lax.broadcasted_iota(jnp.int32, (lanes, tokens), 0)
        group = row // CAP
        slot = row - group * CAP
        label = jnp.zeros((lanes, tokens), jnp.int32)
        for p, k in enumerate(order):
            label = jnp.where(group == p, lax.rem(e + k, ne), label)
        chosen = jnp.zeros((lanes, tokens), F32)
        scale = jnp.zeros((lanes, tokens), F32)
        loads[5].wait()
        loads[6].wait()
        for c in range(top):
            hit = routes[c : c + 1, :] == label
            chosen = chosen + jnp.where(hit, 1.0, 0.0)
            scale = scale + jnp.where(hit, combine[c : c + 1, :], 0.0)
        row_id = lax.broadcasted_iota(jnp.int32, (tokens, tokens), 0)
        col_id = lax.broadcasted_iota(jnp.int32, (tokens, tokens), 1)
        upper = jnp.where(row_id < col_id, 1.0, 0.0).astype(BF16)
        before = dot(chosen.astype(BF16), upper, 1, 0)
        keep = jnp.logical_and(chosen > 0.0, before == slot.astype(F32))
        pick_f = jnp.where(keep, 1.0, 0.0)
        pick = pick_f.astype(BF16)
        factor = jnp.sum(pick_f * scale, axis=1, keepdims=True)

        loads[0].wait()
        loads[1].wait()

        sends = []
        for c, (lo, hi) in enumerate(out_cuts):
            for j in range(nd - 1, -1, -1):
                dj = lax.rem(d + j, nd)
                span = pl.ds(pl.multiple_of(dj * half + lo, 128), hi - lo)
                in_pick = dot(pick, li[:, span], 1, 0)
                gr_pick = dot(pick, go[:, span], 1, 0) * factor
                if not sends:
                    pl.semaphore_wait(barrier, peers)
                for k in range(ne - 1, -1, -1):
                    at = place[k] * CAP
                    tile = jnp.concatenate(
                        [in_pick[at : at + CAP], gr_pick[at : at + CAP]], axis=0
                    ).astype(BF16)
                    b = k * nd + j
                    if j == 0 and k == 0:
                        recv[b, :, lo:hi] = tile
                        continue
                    send[b, :, lo:hi] = tile
                    copy = pltpu.make_async_remote_copy(
                        src_ref=send.at[b, :, pl.ds(lo, hi - lo)],
                        dst_ref=recv.at[b, :, pl.ds(lo, hi - lo)],
                        send_sem=d_send.at[b, c], recv_sem=d_recv.at[b, c],
                        device_id=(dj, lax.rem(e + k, ne), z), device_id_type=MESH,
                    )
                    copy.start()
                    sends.append((c, copy))
        for c in loads[2:5]:
            c.wait()

        every = ne * nd * 2 * CAP
        gate = jnp.zeros((every, hidden), F32)
        up = jnp.zeros((every, hidden), F32)
        dhid = jnp.zeros((every, hidden), F32)
        for c, (lo, hi) in enumerate(out_cuts):
            for part, copy in sends:
                if part == c:
                    copy.wait_recv()
            xc = recv[:, :, lo:hi].reshape(every, hi - lo)
            gate = gate + dot(xc, gw[lo:hi, :], 1, 0)
            up = up + dot(xc, uw[lo:hi, :], 1, 0)
            dhid = dhid + dot(xc, dw[:, lo:hi], 1, 1)

        def take(v, which):
            v = v.reshape(ne * nd, 2, CAP, hidden)[:, which]
            return v.reshape(rows, hidden)

        gate, up, dhid = take(gate, 0), take(up, 0), take(dhid, 1)
        psend[0] = gate.astype(psend.dtype)
        psend[1] = up.astype(psend.dtype)
        psend[2] = dhid.astype(psend.dtype)
        pcopies = []
        for j in range(1, nd):
            c = pltpu.make_async_remote_copy(
                src_ref=psend, dst_ref=precv.at[j - 1],
                send_sem=p_send.at[j - 1], recv_sem=p_recv.at[j - 1],
                device_id=(lax.rem(d + j, nd), e, z), device_id_type=MESH,
            )
            c.start()
            pcopies.append(c)

        def swap(v, j):
            v = v.reshape(ne, nd, CAP, hidden)
            parts = [v[:, (q + nd - j) % nd] for q in range(nd)]
            return jnp.stack(parts, axis=1).reshape(rows, hidden)

        for j, c in enumerate(pcopies, start=1):
            c.wait_recv()
            gate = gate + swap(precv[j - 1, 0].astype(F32), j)
            up = up + swap(precv[j - 1, 1].astype(F32), j)
            dhid = dhid + swap(precv[j - 1, 2].astype(F32), j)

        sigma = jax.nn.sigmoid(gate)
        silu = gate * sigma
        act = silu * up
        d_up = dhid * silu
        d_gate = dhid * up * sigma * (1.0 + gate * (1.0 - sigma))

        def term_copy(k, j, c):
            lo, hi = back_cuts[c]
            span = pl.ds(lo, hi - lo)
            return pltpu.make_async_remote_copy(
                src_ref=rowg.at[k, j, :, span], dst_ref=terms.at[z, k // nz, d, :, span],
                send_sem=r_send.at[k, j, c], recv_sem=r_recv.at[z, k // nz, d, c],
                device_id=(lax.rem(d + nd - j, nd), lax.rem(e + ne - k, ne), k % nz),
                device_id_type=MESH,
            )

        def own_copy(c):
            lo, hi = back_cuts[c]
            span = pl.ds(lo, hi - lo)
            return pltpu.make_async_copy(
                rowg.at[0, 0, :, span], terms.at[0, 0, d, :, span], r_recv.at[0, 0, d, c]
            )

        dg_bf, du_bf = d_gate.astype(BF16), d_up.astype(BF16)
        for c, (lo, hi) in enumerate(back_cuts):
            grad = dot(dg_bf, gw[lo:hi, :], 1, 1) + dot(du_bf, uw[lo:hi, :], 1, 1)
            grad = grad.reshape(ne, nd, CAP, hi - lo)
            for k in range(ne - 1, -1, -1):
                for j in range(nd):
                    rowg[k, j, :, lo:hi] = grad[k, j].astype(BF16)
                    if k == 0 and j == 0:
                        @pl.when(z == 0)
                        def _():
                            own_copy(c).start()

                        @pl.when(z != 0)
                        def _():
                            term_copy(0, 0, c).start()
                    else:
                        term_copy(k, j, c).start()

        def pad(v, which):
            v = v.reshape(ne * nd, CAP, hidden)
            zero = jnp.zeros_like(v)
            pair = [v, zero] if which == 0 else [zero, v]
            return jnp.concatenate(pair, axis=1).reshape(ne * nd * 2 * CAP, hidden).astype(BF16)

        dg_pad = pad(d_gate, 0)
        du_pad = pad(d_up, 0)
        act_pad = pad(act, 1)
        x = recv[...].reshape(every, half)
        gg_ref[0] = (dot(x, dg_pad, 0, 0) * 0.25).astype(BF16)
        gu_ref[0] = (dot(x, du_pad, 0, 0) * 0.25).astype(BF16)
        gd_ref[0] = (dot(act_pad, x, 0, 0) * 0.25).astype(BF16)

        ag = []
        for c, (lo, hi) in enumerate(back_cuts):
            span = pl.ds(lo, hi - lo)
            total = jnp.zeros((ni, nd, CAP, hi - lo), F32)
            for q in range(nz):
                for i in range(ni):
                    for h in range(nd):
                        ref = terms.at[q, i, h, :, span]
                        pltpu.make_async_copy(ref, ref, r_recv.at[q, i, h, c]).wait()
                total = total + terms[q, :, :, :, lo:hi].astype(F32)
            agbuf[z, :, :, :, lo:hi] = total.astype(BF16)
            ref = agbuf.at[z, :, :, :, span]
            for r in range(1, nz):
                copy = pltpu.make_async_remote_copy(
                    src_ref=ref, dst_ref=ref,
                    send_sem=a_send.at[r - 1, c], recv_sem=a_recv.at[r - 1, c],
                    device_id=(d, e, lax.rem(z + r, nz)), device_id_type=MESH,
                )
                copy.start()
                ag.append(copy)

        for c, (lo, hi) in enumerate(back_cuts):
            for r in range(1, nz):
                ref = agbuf.at[lax.rem(z + nz - r, nz), :, :, :, pl.ds(lo, hi - lo)]
                pltpu.make_async_copy(ref, ref, a_recv.at[r - 1, c]).wait()
            for q in range(nd):
                got = agbuf[:, :, q, :, lo:hi].astype(F32).reshape(lanes, hi - lo).astype(BF16)
                out_ref[:, q * half + lo : q * half + hi] = dot(pick, got, 0, 0).astype(BF16)

        for part, copy in sends:
            copy.wait_send()
        for c in pcopies:
            c.wait_send()
        for c in range(len(back_cuts)):
            for k in range(ne):
                for j in range(nd):
                    if k == 0 and j == 0:
                        @pl.when(z != 0)
                        def _():
                            term_copy(0, 0, c).wait_send()
                    else:
                        term_copy(k, j, c).wait_send()
        for c in ag:
            c.wait_send()

    return kernel


def body(grad_out, layer_in, routes, combine, gate_weight, up_weight, down_weight):
    nd = lax.axis_size("dp")
    ne = lax.axis_size("expert")
    nz = lax.axis_size("tensor")
    tokens, width = grad_out.shape
    top = routes.shape[1]
    half, hidden = gate_weight.shape[1:]
    ni = ne // nz
    blocks = ne * nd
    kernel = make_kernel(nd, ne, nz, tokens, width, half, hidden, top)
    hbm = pl.BlockSpec(memory_space=pltpu.HBM)
    vmem = pl.BlockSpec(memory_space=pltpu.VMEM)
    dma = pltpu.SemaphoreType.DMA
    held = 2 * (tokens * width + 3 * half * hidden)
    room = VMEM - held
    parts = pl.pallas_call(
            kernel,
            out_shape=(
                pltpu.VMEM((tokens, width), BF16),
                pltpu.VMEM(gate_weight.shape, BF16),
                pltpu.VMEM(up_weight.shape, BF16),
                pltpu.VMEM(down_weight.shape, BF16),
            ),
            in_specs=[hbm] * 7,
            out_specs=(vmem,) * 4,
            scratch_shapes=[
                pltpu.VMEM((tokens, width), BF16),
                pltpu.VMEM((tokens, width), BF16),
                pltpu.VMEM((top, tokens), jnp.int32),
                pltpu.VMEM((top, tokens), F32),
                pltpu.VMEM((half, hidden), BF16),
                pltpu.VMEM((half, hidden), BF16),
                pltpu.VMEM((hidden, half), BF16),
                pltpu.VMEM((blocks, 2 * CAP, half), BF16),
                pltpu.VMEM((blocks, 2 * CAP, half), BF16),
                pltpu.VMEM((3, blocks * CAP, hidden), BF16),
                pltpu.VMEM((nd - 1, 3, blocks * CAP, hidden), BF16),
                pltpu.VMEM((ne, nd, CAP, half), BF16),
                pltpu.VMEM((nz, ni, nd, CAP, half), BF16),
                pltpu.VMEM((nz, ni, nd, CAP, half), BF16),
                dma((7,)),
                dma((blocks, OUT_PARTS)),
                dma((blocks, OUT_PARTS)),
                dma((nd - 1,)),
                dma((nd - 1,)),
                dma((ne, nd, BACK_PARTS)),
                dma((nz, ni, nd, BACK_PARTS)),
                dma((nz - 1, BACK_PARTS)),
                dma((nz - 1, BACK_PARTS)),
            ],
            compiler_params=pltpu.CompilerParams(
                collective_id=0, has_side_effects=True, vmem_limit_bytes=room
            ),
        )(grad_out, layer_in, routes.T, combine.T, gate_weight, up_weight, down_weight)
    return tuple(parts)


def solution(mesh):
    return jax.shard_map(
        body,
        mesh=mesh,
        in_specs=(
            P(("dp", "expert"), None),
            P(("dp", "expert"), None),
            P(("dp", "expert"), None),
            P(("dp", "expert"), None),
            P("expert", "dp", "tensor"),
            P("expert", "dp", "tensor"),
            P("expert", "tensor", "dp"),
        ),
        out_specs=(
            P(("dp", "expert"), None),
            P("expert", "dp", "tensor"),
            P("expert", "dp", "tensor"),
            P("expert", "tensor", "dp"),
        ),
        check_vma=False,
    )
```

```python
import jax
import jax.numpy as jnp
from jax import lax
from jax.experimental import pallas as pl
from jax.experimental.pallas import tpu as pltpu
from jax.sharding import PartitionSpec as P

CAP = 8
OUT_PARTS = 2
BACK_PARTS = 2
VMEM = 67043328
MESH = pl.DeviceIdType.MESH
F32 = jnp.float32
BF16 = jnp.bfloat16


def dot(a, b, ca, cb):
    return lax.dot_general(a, b, (((ca,), (cb,)), ((), ())), preferred_element_type=F32)


def cuts(extent, parts):
    tiles = extent // 128
    edges = [128 * ((tiles * c + parts - 1) // parts) for c in range(parts + 1)]
    return list(zip(edges[:-1], edges[1:]))


def make_kernel(nd, ne, nz, tokens, width, half, hidden, top):
    ni = ne // nz
    order = [z + nz * i for z in range(nz) for i in range(ni)]
    place = {k: p for p, k in enumerate(order)}
    lanes = ne * CAP
    rows = ne * nd * CAP
    out_cuts = cuts(half, OUT_PARTS)
    back_cuts = cuts(half, BACK_PARTS)

    def kernel(
        go_hbm, li_hbm, routes_hbm, combine_hbm, gw_hbm, uw_hbm, dw_hbm,
        out_ref, gg_ref, gu_ref, gd_ref,
        go, li, routes, combine, gw, uw, dw, send, recv, psend, precv, rowg, terms, agbuf,
        ld_sem, d_send, d_recv, p_send, p_recv, r_send, r_recv,
        a_send, a_recv,
    ):
        d = lax.axis_index("dp")
        e = lax.axis_index("expert")
        z = lax.axis_index("tensor")

        loads = [
            pltpu.make_async_copy(li_hbm, li, ld_sem.at[0]),
            pltpu.make_async_copy(go_hbm, go, ld_sem.at[1]),
            pltpu.make_async_copy(gw_hbm.at[0], gw, ld_sem.at[2]),
            pltpu.make_async_copy(uw_hbm.at[0], uw, ld_sem.at[3]),
            pltpu.make_async_copy(dw_hbm.at[0], dw, ld_sem.at[4]),
            pltpu.make_async_copy(routes_hbm, routes, ld_sem.at[5]),
            pltpu.make_async_copy(combine_hbm, combine, ld_sem.at[6]),
        ]
        for i in (5, 6, 0, 1, 2, 3, 4):
            loads[i].start()

        barrier = pltpu.get_barrier_semaphore()
        peers = 0
        for r in range(1, nz):
            pl.semaphore_signal(
                barrier, inc=1, device_id=(d, e, lax.rem(z + r, nz)), device_id_type=MESH
            )
            peers += 1
        for k in range(ne - 1, -1, -1):
            for j in range(nd):
                if j == 0 and k == 0:
                    continue
                pl.semaphore_signal(
                    barrier, inc=1,
                    device_id=(lax.rem(d + j, nd), lax.rem(e + k, ne), z),
                    device_id_type=MESH,
                )
                peers += 1

        row = lax.broadcasted_iota(jnp.int32, (lanes, tokens), 0)
        group = row // CAP
        slot = row - group * CAP
        label = jnp.zeros((lanes, tokens), jnp.int32)
        for p, k in enumerate(order):
            label = jnp.where(group == p, lax.rem(e + k, ne), label)
        chosen = jnp.zeros((lanes, tokens), F32)
        scale = jnp.zeros((lanes, tokens), F32)
        loads[5].wait()
        loads[6].wait()
        for c in range(top):
            hit = routes[c : c + 1, :] == label
            chosen = chosen + jnp.where(hit, 1.0, 0.0)
            scale = scale + jnp.where(hit, combine[c : c + 1, :], 0.0)
        row_id = lax.broadcasted_iota(jnp.int32, (tokens, tokens), 0)
        col_id = lax.broadcasted_iota(jnp.int32, (tokens, tokens), 1)
        upper = jnp.where(row_id < col_id, 1.0, 0.0).astype(BF16)
        before = dot(chosen.astype(BF16), upper, 1, 0)
        keep = jnp.logical_and(chosen > 0.0, before == slot.astype(F32))
        pick_f = jnp.where(keep, 1.0, 0.0)
        pick = pick_f.astype(BF16)
        factor = jnp.sum(pick_f * scale, axis=1, keepdims=True)

        loads[0].wait()
        loads[1].wait()

        sends = []
        for c, (lo, hi) in enumerate(out_cuts):
            for j in range(nd - 1, -1, -1):
                dj = lax.rem(d + j, nd)
                span = pl.ds(pl.multiple_of(dj * half + lo, 128), hi - lo)
                in_pick = dot(pick, li[:, span], 1, 0)
                gr_pick = dot(pick, go[:, span], 1, 0) * factor
                if not sends:
                    pl.semaphore_wait(barrier, peers)
                for k in range(ne - 1, -1, -1):
                    at = place[k] * CAP
                    tile = jnp.concatenate(
                        [in_pick[at : at + CAP], gr_pick[at : at + CAP]], axis=0
                    ).astype(BF16)
                    b = k * nd + j
                    if j == 0 and k == 0:
                        recv[b, :, lo:hi] = tile
                        continue
                    send[b, :, lo:hi] = tile
                    copy = pltpu.make_async_remote_copy(
                        src_ref=send.at[b, :, pl.ds(lo, hi - lo)],
                        dst_ref=recv.at[b, :, pl.ds(lo, hi - lo)],
                        send_sem=d_send.at[b, c], recv_sem=d_recv.at[b, c],
                        device_id=(dj, lax.rem(e + k, ne), z), device_id_type=MESH,
                    )
                    copy.start()
                    sends.append((c, copy))
        for c in loads[2:5]:
            c.wait()

        every = ne * nd * 2 * CAP
        gate = jnp.zeros((every, hidden), F32)
        up = jnp.zeros((every, hidden), F32)
        dhid = jnp.zeros((every, hidden), F32)
        for c, (lo, hi) in enumerate(out_cuts):
            for part, copy in sends:
                if part == c:
                    copy.wait_recv()
            xc = recv[:, :, lo:hi].reshape(every, hi - lo)
            gate = gate + dot(xc, gw[lo:hi, :], 1, 0)
            up = up + dot(xc, uw[lo:hi, :], 1, 0)
            dhid = dhid + dot(xc, dw[:, lo:hi], 1, 1)

        def take(v, which):
            v = v.reshape(ne * nd, 2, CAP, hidden)[:, which]
            return v.reshape(rows, hidden)

        gate, up, dhid = take(gate, 0), take(up, 0), take(dhid, 1)
        psend[0] = gate.astype(psend.dtype)
        psend[1] = up.astype(psend.dtype)
        psend[2] = dhid.astype(psend.dtype)
        pcopies = []
        for j in range(1, nd):
            c = pltpu.make_async_remote_copy(
                src_ref=psend, dst_ref=precv.at[j - 1],
                send_sem=p_send.at[j - 1], recv_sem=p_recv.at[j - 1],
                device_id=(lax.rem(d + j, nd), e, z), device_id_type=MESH,
            )
            c.start()
            pcopies.append(c)

        def swap(v, j):
            v = v.reshape(ne, nd, CAP, hidden)
            parts = [v[:, (q + nd - j) % nd] for q in range(nd)]
            return jnp.stack(parts, axis=1).reshape(rows, hidden)

        for j, c in enumerate(pcopies, start=1):
            c.wait_recv()
            gate = gate + swap(precv[j - 1, 0].astype(F32), j)
            up = up + swap(precv[j - 1, 1].astype(F32), j)
            dhid = dhid + swap(precv[j - 1, 2].astype(F32), j)

        sigma = jax.nn.sigmoid(gate)
        silu = gate * sigma
        act = silu * up
        d_up = dhid * silu
        d_gate = dhid * up * sigma * (1.0 + gate * (1.0 - sigma))

        def term_copy(k, j, c):
            lo, hi = back_cuts[c]
            span = pl.ds(lo, hi - lo)
            return pltpu.make_async_remote_copy(
                src_ref=rowg.at[k, j, :, span], dst_ref=terms.at[z, k // nz, d, :, span],
                send_sem=r_send.at[k, j, c], recv_sem=r_recv.at[z, k // nz, d, c],
                device_id=(lax.rem(d + nd - j, nd), lax.rem(e + ne - k, ne), k % nz),
                device_id_type=MESH,
            )

        def own_copy(c):
            lo, hi = back_cuts[c]
            span = pl.ds(lo, hi - lo)
            return pltpu.make_async_copy(
                rowg.at[0, 0, :, span], terms.at[0, 0, d, :, span], r_recv.at[0, 0, d, c]
            )

        dg_bf, du_bf = d_gate.astype(BF16), d_up.astype(BF16)
        for c, (lo, hi) in enumerate(back_cuts):
            grad = dot(dg_bf, gw[lo:hi, :], 1, 1) + dot(du_bf, uw[lo:hi, :], 1, 1)
            grad = grad.reshape(ne, nd, CAP, hi - lo)
            for k in range(ne - 1, -1, -1):
                for j in range(nd):
                    rowg[k, j, :, lo:hi] = grad[k, j].astype(BF16)
                    if k == 0 and j == 0:
                        @pl.when(z == 0)
                        def _():
                            own_copy(c).start()

                        @pl.when(z != 0)
                        def _():
                            term_copy(0, 0, c).start()
                    else:
                        term_copy(k, j, c).start()

        def pad(v, which):
            v = v.reshape(ne * nd, CAP, hidden)
            zero = jnp.zeros_like(v)
            pair = [v, zero] if which == 0 else [zero, v]
            return jnp.concatenate(pair, axis=1).reshape(ne * nd * 2 * CAP, hidden).astype(BF16)

        dg_pad = pad(d_gate, 0)
        du_pad = pad(d_up, 0)
        act_pad = pad(act, 1)
        x = recv[...].reshape(every, half)
        gg_ref[0] = (dot(x, dg_pad, 0, 0) * 0.25).astype(BF16)
        gu_ref[0] = (dot(x, du_pad, 0, 0) * 0.25).astype(BF16)
        gd_ref[0] = (dot(act_pad, x, 0, 0) * 0.25).astype(BF16)

        ag = []
        for c, (lo, hi) in enumerate(back_cuts):
            span = pl.ds(lo, hi - lo)
            total = jnp.zeros((ni, nd, CAP, hi - lo), F32)
            for q in range(nz):
                for i in range(ni):
                    for h in range(nd):
                        ref = terms.at[q, i, h, :, span]
                        pltpu.make_async_copy(ref, ref, r_recv.at[q, i, h, c]).wait()
                total = total + terms[q, :, :, :, lo:hi].astype(F32)
            agbuf[z, :, :, :, lo:hi] = total.astype(BF16)
            ref = agbuf.at[z, :, :, :, span]
            for r in range(1, nz):
                copy = pltpu.make_async_remote_copy(
                    src_ref=ref, dst_ref=ref,
                    send_sem=a_send.at[r - 1, c], recv_sem=a_recv.at[r - 1, c],
                    device_id=(d, e, lax.rem(z + r, nz)), device_id_type=MESH,
                )
                copy.start()
                ag.append(copy)

        for c, (lo, hi) in enumerate(back_cuts):
            for r in range(1, nz):
                ref = agbuf.at[lax.rem(z + nz - r, nz), :, :, :, pl.ds(lo, hi - lo)]
                pltpu.make_async_copy(ref, ref, a_recv.at[r - 1, c]).wait()
            for q in range(nd):
                got = agbuf[:, :, q, :, lo:hi].astype(F32).reshape(lanes, hi - lo).astype(BF16)
                out_ref[:, q * half + lo : q * half + hi] = dot(pick, got, 0, 0).astype(BF16)

        for part, copy in sends:
            copy.wait_send()
        for c in pcopies:
            c.wait_send()
        for c in range(len(back_cuts)):
            for k in range(ne):
                for j in range(nd):
                    if k == 0 and j == 0:
                        @pl.when(z != 0)
                        def _():
                            term_copy(0, 0, c).wait_send()
                    else:
                        term_copy(k, j, c).wait_send()
        for c in ag:
            c.wait_send()

    return kernel


def body(grad_out, layer_in, routes, combine, gate_weight, up_weight, down_weight):
    nd = lax.axis_size("dp")
    ne = lax.axis_size("expert")
    nz = lax.axis_size("tensor")
    tokens, width = grad_out.shape
    top = routes.shape[1]
    half, hidden = gate_weight.shape[1:]
    ni = ne // nz
    blocks = ne * nd
    kernel = make_kernel(nd, ne, nz, tokens, width, half, hidden, top)
    hbm = pl.BlockSpec(memory_space=pltpu.HBM)
    vmem = pl.BlockSpec(memory_space=pltpu.VMEM)
    dma = pltpu.SemaphoreType.DMA
    held = 2 * (tokens * width + 3 * half * hidden)
    room = VMEM - held
    parts = pl.pallas_call(
            kernel,
            out_shape=(
                pltpu.VMEM((tokens, width), BF16),
                pltpu.VMEM(gate_weight.shape, BF16),
                pltpu.VMEM(up_weight.shape, BF16),
                pltpu.VMEM(down_weight.shape, BF16),
            ),
            in_specs=[hbm] * 7,
            out_specs=(vmem,) * 4,
            scratch_shapes=[
                pltpu.VMEM((tokens, width), BF16),
                pltpu.VMEM((tokens, width), BF16),
                pltpu.VMEM((top, tokens), jnp.int32),
                pltpu.VMEM((top, tokens), F32),
                pltpu.VMEM((half, hidden), BF16),
                pltpu.VMEM((half, hidden), BF16),
                pltpu.VMEM((hidden, half), BF16),
                pltpu.VMEM((blocks, 2 * CAP, half), BF16),
                pltpu.VMEM((blocks, 2 * CAP, half), BF16),
                pltpu.VMEM((3, blocks * CAP, hidden), BF16),
                pltpu.VMEM((nd - 1, 3, blocks * CAP, hidden), BF16),
                pltpu.VMEM((ne, nd, CAP, half), BF16),
                pltpu.VMEM((nz, ni, nd, CAP, half), BF16),
                pltpu.VMEM((nz, ni, nd, CAP, half), BF16),
                dma((7,)),
                dma((blocks, OUT_PARTS)),
                dma((blocks, OUT_PARTS)),
                dma((nd - 1,)),
                dma((nd - 1,)),
                dma((ne, nd, BACK_PARTS)),
                dma((nz, ni, nd, BACK_PARTS)),
                dma((nz - 1, BACK_PARTS)),
                dma((nz - 1, BACK_PARTS)),
            ],
            compiler_params=pltpu.CompilerParams(
                collective_id=0, has_side_effects=True, vmem_limit_bytes=room
            ),
        )(grad_out, layer_in, routes.T, combine.T, gate_weight, up_weight, down_weight)
    return tuple(parts)


def solution(mesh):
    return jax.shard_map(
        body,
        mesh=mesh,
        in_specs=(
            P(("dp", "expert"), None),
            P(("dp", "expert"), None),
            P(("dp", "expert"), None),
            P(("dp", "expert"), None),
            P("expert", "dp", "tensor"),
            P("expert", "dp", "tensor"),
            P("expert", "tensor", "dp"),
        ),
        out_specs=(
            P(("dp", "expert"), None),
            P("expert", "dp", "tensor"),
            P("expert", "dp", "tensor"),
            P("expert", "tensor", "dp"),
        ),
        check_vma=False,
    )
```
